32 devices in a mesh: seq: 8 (over y, x, core), head: 4 (over z).
Axes of the slice: x: 2, y: 2, z: 4, core: 2. Of those that a mesh axis runs over, the one named last changes fastest.
Arguments:
- query: bfloat16 [2048, 4096], P('seq', 'head'), may hold values from -6 to 6
- key: bfloat16 [2048, 4096], P('seq', 'head'), may hold values from -6 to 6
- value: bfloat16 [2048, 4096], P('seq', 'head'), may hold values from -6 to 6
- head_gain: float32 [4096], P('head'), may hold values from 0.1 to 1.9
- out_weight: bfloat16 [4096, 4096], P('head', 'seq'), may hold values from -0.09375 to 0.09375
- stream: bfloat16 [2048, 4096], P(('seq', 'head')), may hold values from -6 to 6
- model_gain: float32 [4096], replicated, may hold values from 0.1 to 1.9
- expert_ids: int32 [2048, 8], P(('seq', 'head')), may hold values from 0 to 31, all different within a row; in each aligned block of 64 rows (0 to 63, 64 to 127, ...) at most 24 rows name the same one
- expert_gates: float32 [2048, 8], P(('seq', 'head')), may hold values from 0.1 to 0.5
- gate_weight: bfloat16 [32, 4096, 768], P(('seq', 'head')), may hold values from -0.09375 to 0.09375
- up_weight: bfloat16 [32, 4096, 768], P(('seq', 'head')), may hold values from -0.09375 to 0.09375
- down_weight: bfloat16 [32, 768, 4096], P(('seq', 'head')), may hold values from -0.21875 to 0.21875
- weight_scales: float32 [32, 3], P(('seq', 'head')), may hold values from 0.6 to 1.6
Outputs:
- layer_out: bfloat16 [2048, 4096], P(('seq', 'head'))
The draws below stay inside these ranges and needn't reach their ends.
Inputs may be any that keep to these rules, and one draw needn't show every extreme that they name: `expert_ids`: among the 64 tokens of one device (aligned blocks of rows), no expert is named more than 24 times, a bound that some block reaches; the entries of one row differ.
All inputs are finite; a program needn't handle non-finite values.
Results may differ from the reference program's by a relative error of at most 0.013.
Values may be sent and summed in bfloat16 or wider, within the bound.
A program may use at most 128 MiB of HBM per device.

```python
import math
import jax
import jax.numpy as jnp
import numpy as np
from jax import lax

D = 4096
HEADS = 32
HD = 128
FF = 768
TOPK = 8
SEQ_DEV = 256
TOK_DEV = 64
EXPERTS = 32
CAP = 24
TOKENS = 2048
N_SEQ = 8
N_HEAD = 4


def shard_levels(rng, dims, split, smallest, top_value):
    factor_of, own = 1.0, jax.random.fold_in(rng, 6)
    for axis_at, parts in split:
        heights = jnp.exp(jax.random.uniform(jax.random.fold_in(own, axis_at), (parts,), jnp.float32, smallest / len(split), top_value / len(split)))
        factor_of = factor_of * jnp.repeat(heights, dims[axis_at] // parts).reshape([-1 if axis == axis_at else 1 for axis in range(len(dims))])
    return factor_of


def shared_out(rng, own, number, rows, count, top, bound, lean):
    order = jax.random.permutation(rng, count)
    packed, usual = shares(count, rows * top, bound, lean, True), shares(count, rows * top, bound, lean, False)
    places = jnp.arange(count)

    def named(tallies, rotation):
        used = int((tallies > 0).sum())
        fixed = max(1, used // 4)
        passed = fixed + (places - fixed + rotation * (used - fixed)) % max(1, count - fixed)
        return jnp.zeros((count,), jnp.int32).at[order[jnp.where(places < fixed, places, passed)]].set(jnp.asarray(tallies, jnp.int32))

    tallies = jnp.where(number % 4 == 0, named(packed, number // 4), named(usual, number - number // 4 - 1))
    mixed = jax.random.permutation(jax.random.fold_in(own, 3), count)
    donor, receiver = mixed[0:count // 2 * 2:2], mixed[1:count // 2 * 2:2]
    margin = jnp.minimum(tallies[donor] - 1, bound - tallies[receiver]) // 2
    margin = jnp.where((donor == order[0]) | (receiver == order[0]) | (tallies[receiver] == 0), 0, jnp.maximum(margin, 0))
    passed = jax.random.randint(jax.random.fold_in(own, 4), (count // 2,), 0, 1 << 20) % (margin + 1)
    tallies = tallies.at[donor].add(-passed).at[receiver].add(passed)
    members = jnp.searchsorted(jnp.cumsum(tallies), jnp.arange(rows * top), side="right").astype(jnp.int32)
    listing = members.reshape(top, rows).T
    listing = listing[jax.random.permutation(jax.random.fold_in(own, 1), rows)]
    rotation = jax.random.randint(jax.random.fold_in(own, 2), (rows, 1), 0, top)
    return jnp.take_along_axis(listing, (jnp.arange(top)[None, :] + rotation) % top, axis=1)


def shares(count, total, most, lean, full):
    portions = [(1 << 20) // math.isqrt(standing ** lean) + 1 for standing in range(1, count + 1)]
    largest = most if full else min(most, max(-(-total // count), total * portions[0] // sum(portions)))
    least = 1 if total - largest >= count - 1 else 0
    given, spare = [largest] + [least] * (count - 1), total - largest - least * (count - 1)
    while spare > 0:
        candidates = [i for i in range(1, count) if given[i] < largest] or [i for i in range(1, count) if given[i] < most]
        mass, remaining = sum([portions[i] for i in candidates]), spare
        for i in candidates:
            more = min(most - given[i], max(1, remaining * portions[i] // mass), spare)
            given[i] = given[i] + more
            spare = spare - more
    return np.array(given)


def normal_values(key, shape, width, reach, pieces=(), kind=jnp.bfloat16):
    result = jax.random.normal(key, shape, jnp.float32) * width
    if len(pieces) > 0:
        result = shard_levels(key, shape, pieces, -0.22, 0.18) * result
    return jnp.clip(result, min=-reach, max=reach).astype(kind)


def setup_inputs(seed: int = 0) -> dict:
    key_list = jax.random.split(jax.random.key(seed), 14)
    query = normal_values(key_list[0], (TOKENS, HEADS * HD), 1.0, 6.0, ((0, 8), (1, 4)))
    key = normal_values(key_list[1], (TOKENS, HEADS * HD), 1.0, 6.0, ((0, 8), (1, 4)))
    value = normal_values(key_list[2], (TOKENS, HEADS * HD), 1.0, 6.0, ((0, 8), (1, 4)))
    head_gain = jnp.clip(1.0 + 0.18 * jax.random.normal(key_list[3], (HEADS * HD,), jnp.float32), 0.1, 1.9)
    out_weight = normal_values(key_list[4], (HEADS * HD, D), (HEADS * HD) ** -0.5, 0.09375, ((0, 4), (1, 8)))
    stream = normal_values(key_list[5], (TOKENS, D), 1.0, 6.0, ((0, 32),))
    model_gain = jnp.clip(1.0 + 0.18 * jax.random.normal(key_list[6], (D,), jnp.float32), 0.1, 1.9)
    expert_ids_keys = jax.random.split(jax.random.fold_in(key_list[7], 1), TOKENS // TOK_DEV)
    expert_ids_turns = jax.random.permutation(jax.random.fold_in(key_list[7], 3), TOKENS // TOK_DEV)
    expert_ids = jax.vmap(lambda own, number: shared_out(jax.random.fold_in(key_list[7], 2), own, number, TOK_DEV, EXPERTS, TOPK, CAP, 2))(expert_ids_keys, expert_ids_turns).reshape((TOKENS, TOPK))
    expert_gates = jnp.clip(0.1 + 0.4 * jax.random.uniform(key_list[8], (TOKENS, TOPK), jnp.float32) ** shard_levels(key_list[8], (TOKENS, TOPK), ((0, 32),), -0.2, 0.2), 0.1, 0.5)
    gate_weight = normal_values(key_list[9], (EXPERTS, D, FF), D ** -0.5, 0.09375, ((0, 32),))
    up_weight = normal_values(key_list[10], (EXPERTS, D, FF), D ** -0.5, 0.09375, ((0, 32),))
    down_weight = normal_values(key_list[11], (EXPERTS, FF, D), FF ** -0.5, 0.21875, ((0, 32),))
    weight_scales = jnp.clip(jnp.exp(math.log(1.6) - 0.98082923 * jax.random.uniform(key_list[12], (EXPERTS, 3), jnp.float32) ** shard_levels(key_list[12], (EXPERTS, 3), ((0, 32),), -0.2, 0.2)), 0.6, 1.6)
    return dict(query=query, key=key, value=value, head_gain=head_gain, out_weight=out_weight, stream=stream, model_gain=model_gain, expert_ids=expert_ids, expert_gates=expert_gates, gate_weight=gate_weight, up_weight=up_weight, down_weight=down_weight, weight_scales=weight_scales)


def to_bf16_value(array):
    return lax.optimization_barrier(array.astype(jnp.bfloat16)).astype(jnp.float32)

def reference(query, key, value, head_gain, out_weight, stream, model_gain, expert_ids, expert_gates, gate_weight, up_weight, down_weight, weight_scales):
    query_blocks = query.reshape(N_SEQ, SEQ_DEV, HEADS, HD)
    key_blocks = key.reshape(N_SEQ, SEQ_DEV, HEADS, HD)
    value_blocks = value.reshape(N_SEQ, SEQ_DEV, HEADS, HD)
    causal = jnp.tril(jnp.ones((SEQ_DEV, SEQ_DEV), dtype=bool))

    def block_step(carried, slices):
        query_rows, key_rows, value_rows = slices
        query_float = query_rows.astype(jnp.float32)
        key_float = key_rows.astype(jnp.float32)
        value_float = value_rows.astype(jnp.float32)
        scores = jnp.einsum('thd,shd->hts', query_float, key_float)
        scores = to_bf16_value(jnp.where(causal[None, :, :], scores, 0.0))
        local_part = jnp.einsum('hts,shd->thd', scores, value_float)
        prior_state = to_bf16_value(carried)
        earlier_part = jnp.einsum('thd,hde->the', query_float, prior_state)
        updated = carried + jnp.einsum('shd,she->hde', key_float, value_float)
        return (updated, local_part + earlier_part)
    initial = jnp.zeros((HEADS, HD, HD), jnp.float32)
    final_state, mixed_heads = lax.scan(block_step, initial, (query_blocks, key_blocks, value_blocks))
    mixed_heads = mixed_heads.reshape(TOKENS, HEADS, HD)
    mean_square = lax.optimization_barrier(jnp.mean(mixed_heads * mixed_heads, axis=-1, keepdims=True))
    head_normed = (mixed_heads * lax.rsqrt(mean_square + 1e-06) * head_gain.reshape(HEADS, HD)).astype(jnp.bfloat16)
    head_normed = head_normed.reshape(TOKENS, HEADS * HD)
    attention = jnp.dot(head_normed.astype(jnp.float32), out_weight.astype(jnp.float32))
    residual = (stream.astype(jnp.float32) + attention).astype(jnp.bfloat16)
    residual_float = residual.astype(jnp.float32)
    mean_square = lax.optimization_barrier(jnp.mean(residual_float * residual_float, axis=-1, keepdims=True))
    normed = (residual_float * lax.rsqrt(mean_square + 1e-06) * model_gain).astype(jnp.bfloat16)
    most_rows = CAP * N_SEQ * N_HEAD

    def expert_step(expert_mix, slices):
        expert, gate_matrix, up_matrix, down_matrix, scale_row = slices
        chosen = expert_ids == expert
        token_weight = lax.optimization_barrier(jnp.sum(jnp.where(chosen, expert_gates, 0.0), axis=1))
        has_expert = jnp.any(chosen, axis=1)
        row_index = jnp.nonzero(has_expert, size=most_rows, fill_value=0)[0].astype(jnp.int32)
        live_count = jnp.sum(has_expert.astype(jnp.int32))
        is_live = (jnp.arange(most_rows, dtype=jnp.int32) < live_count).astype(jnp.float32)
        inputs = normed[row_index].astype(jnp.float32)
        gate_part = jnp.dot(inputs, gate_matrix.astype(jnp.float32)) * scale_row[0]
        up_part = jnp.dot(inputs, up_matrix.astype(jnp.float32)) * scale_row[1]
        act = to_bf16_value(jax.nn.silu(gate_part) * up_part)
        expert_rows = to_bf16_value(jnp.dot(act, down_matrix.astype(jnp.float32)) * scale_row[2])
        weighted = expert_rows * (token_weight[row_index] * is_live)[:, None]
        return (expert_mix.at[row_index].add(weighted), None)
    expert_list = jnp.arange(EXPERTS, dtype=jnp.int32)
    expert_mix, unused = lax.scan(expert_step, jnp.zeros((TOKENS, D), jnp.float32), (expert_list, gate_weight, up_weight, down_weight, weight_scales))
    return (residual_float + expert_mix).astype(jnp.bfloat16)
```

```python
import functools

import jax
import jax.numpy as jnp
from jax import lax
from jax.experimental import pallas as pl
from jax.experimental.pallas import tpu as pltpu
from jax.sharding import PartitionSpec as P

HD = 128
TOPK = 8
MESH = pl.DeviceIdType.MESH


def expert_kernel(
    seqs,
    heads,
    chunks,
    scale_ref,
    x_ref,
    res_ref,
    pick_ref,
    mix_ref,
    gate_hbm,
    up_hbm,
    down_hbm,
    out_ref,
    gate_v,
    up_v,
    down_v,
    gath,
    send,
    recv,
    back,
    acc_g,
    acc_u,
    act,
    part,
    psend,
    precv,
    wsem,
    zs,
    zr,
    ps,
    pr,
    rs,
    rr,
    cs,
    cr,
    lsem,
):
    s = lax.axis_index("seq")
    h = lax.axis_index("head")
    rows, width = x_ref.shape
    step = width // chunks
    slots = send.shape[1]
    block = heads * rows

    def cols(c):
        return pl.ds(pl.multiple_of(c * step, step), step)

    def plane(d):
        return lax.rem(s + d, seqs)

    def line(d):
        return lax.rem(h + d, heads)

    def weights(c):
        return (
            pltpu.make_async_copy(gate_hbm.at[0, cols(c), :], gate_v.at[cols(c), :], wsem.at[0, c]),
            pltpu.make_async_copy(up_hbm.at[0, cols(c), :], up_v.at[cols(c), :], wsem.at[1, c]),
            pltpu.make_async_copy(down_hbm.at[0, :, cols(c)], down_v.at[:, cols(c)], wsem.at[2, c]),
        )

    def remote(src, dst, ssem, rsem, seq, head):
        return pltpu.make_async_remote_copy(
            src_ref=src,
            dst_ref=dst,
            send_sem=ssem,
            recv_sem=rsem,
            device_id=(seq, head),
            device_id_type=MESH,
        )

    barrier = pltpu.get_barrier_semaphore()
    for d in range(1, seqs):
        pl.semaphore_signal(barrier, inc=1, device_id=(plane(d), h), device_id_type=MESH)
    for d in range(1, heads):
        pl.semaphore_signal(barrier, inc=1, device_id=(s, line(d)), device_id_type=MESH)

    def start_weights(c, carry):
        gate, up, _ = weights(c)
        gate.start()
        up.start()
        return carry

    def start_down(c, carry):
        weights(c)[2].start()
        return carry

    lax.fori_loop(0, chunks, start_weights, 0)
    lax.fori_loop(0, chunks, start_down, 0)
    gath[h] = x_ref[...]
    pl.semaphore_wait(barrier, seqs + heads - 2)

    def gather_copy(c, d, source, target):
        return remote(
            x_ref.at[:, cols(c)],
            gath.at[source, :, cols(c)],
            zs.at[c, d],
            zr.at[c, source],
            s,
            target,
        )

    def start_gather(c, carry):
        for d in range(1, heads):
            gather_copy(c, d, h, line(d)).start()
        return carry

    lax.fori_loop(0, chunks, start_gather, 0)

    def plane_copy(c, d):
        return remote(
            send.at[plane(d), :, cols(c)], recv.at[s, :, cols(c)], ps.at[c, d], pr.at[c, s],
            plane(d), h,
        )

    def plane_arrival(c, source):
        return remote(
            send.at[source, :, cols(c)], recv.at[source, :, cols(c)], ps.at[c, 0], pr.at[c, source],
            source, h,
        )

    def own_copy(c):
        return pltpu.make_async_copy(
            send.at[s, :, cols(c)], recv.at[s, :, cols(c)], lsem.at[0, c]
        )

    def pick(c):
        for d in range(1, heads):
            gather_copy(c, d, line(d), line(d)).wait_recv()
        picked = jnp.dot(
            pick_ref[...],
            gath[:, :, cols(c)].reshape(block, step),
            preferred_element_type=jnp.float32,
        )
        send[:, :, cols(c)] = picked.astype(jnp.bfloat16).reshape(seqs, slots, step)
        for d in range(1, seqs):
            plane_copy(c, d).start()
        own_copy(c).start()

    acc_g[...] = jnp.zeros_like(acc_g)
    acc_u[...] = jnp.zeros_like(acc_u)

    def expand(c):
        gate, up, _ = weights(c)
        gate.wait()
        up.wait()
        for d in range(1, seqs):
            plane_arrival(c, plane(d)).wait_recv()
        own_copy(c).wait()
        lhs = recv[:, :, cols(c)].reshape(seqs * slots, step)
        acc_g[...] += jnp.dot(lhs, gate_v[cols(c), :], preferred_element_type=jnp.float32)
        acc_u[...] += jnp.dot(lhs, up_v[cols(c), :], preferred_element_type=jnp.float32)

    pick(0)

    def forward(c, carry):
        pick(c)
        expand(c - 1)
        return carry

    lax.fori_loop(1, chunks, forward, 0)
    expand(chunks - 1)

    gate_scale = scale_ref[0, 0]
    up_scale = scale_ref[0, 1]
    down_scale = scale_ref[0, 2]

    def activate(i, carry):
        at = pl.ds(pl.multiple_of(i * slots, slots), slots)
        g = acc_g[at, :] * gate_scale
        act[at, :] = (g / (1.0 + jnp.exp(-g)) * (acc_u[at, :] * up_scale)).astype(jnp.bfloat16)
        return carry

    lax.fori_loop(0, seqs, activate, 0)

    def back_copy(c, d):
        return remote(
            recv.at[plane(d), :, cols(c)], back.at[s, :, cols(c)], rs.at[c, d], rr.at[c, s],
            plane(d), h,
        )

    def back_arrival(c, source):
        return remote(
            recv.at[source, :, cols(c)], back.at[source, :, cols(c)], rs.at[c, 0], rr.at[c, source],
            source, h,
        )

    def own_back(c):
        return pltpu.make_async_copy(
            recv.at[s, :, cols(c)], back.at[s, :, cols(c)], lsem.at[1, c]
        )

    def sum_copy(c, d):
        return remote(
            psend.at[line(d), :, cols(c)], precv.at[h, :, cols(c)], cs.at[c, d], cr.at[c, h],
            s, line(d),
        )

    def sum_arrival(c, source):
        return remote(
            psend.at[source, :, cols(c)], precv.at[source, :, cols(c)], cs.at[c, 0], cr.at[c, source],
            s, source,
        )

    def contract(c):
        weights(c)[2].wait()
        rows_out = jnp.dot(act[...], down_v[:, cols(c)], preferred_element_type=jnp.float32)
        recv[:, :, cols(c)] = (
            (rows_out * down_scale).astype(jnp.bfloat16).reshape(seqs, slots, step)
        )
        for d in range(1, seqs):
            back_copy(c, d).start()
        own_back(c).start()

    def combine(c):
        for d in range(1, seqs):
            back_arrival(c, plane(d)).wait_recv()
        own_back(c).wait()
        total = jnp.dot(
            mix_ref[...],
            back[:, :, cols(c)].reshape(seqs * slots, step),
            preferred_element_type=jnp.float32,
        ).reshape(heads, rows, step)
        part[:, :, cols(c)] = total
        psend[:, :, cols(c)] = total.astype(jnp.bfloat16)
        for d in range(1, heads):
            sum_copy(c, d).start()

    def finish(c):
        total = res_ref[:, cols(c)].astype(jnp.float32) + part[h, :, cols(c)]
        for d in range(1, heads):
            sum_arrival(c, line(d)).wait_recv()
            total = total + precv[line(d), :, cols(c)].astype(jnp.float32)
        out_ref[:, cols(c)] = total.astype(jnp.bfloat16)

    def run_contract(c, carry):
        contract(c)
        return carry

    def run_combine(c, carry):
        combine(c)
        return carry

    def run_finish(c, carry):
        finish(c)
        return carry

    def drain(c, carry):
        for d in range(1, heads):
            gather_copy(c, d, h, line(d)).wait_send()
            sum_copy(c, d).wait_send()
        for d in range(1, seqs):
            plane_copy(c, d).wait_send()
            back_copy(c, d).wait_send()
        return carry

    lax.fori_loop(0, chunks, run_contract, 0)
    lax.fori_loop(0, chunks, run_combine, 0)
    lax.fori_loop(0, chunks, run_finish, 0)
    lax.fori_loop(0, chunks, drain, 0)


def experts_call(seqs, heads, scales, normed, residual, pick, mix, gate, up, down):
    rows, width = normed.shape
    hidden = gate.shape[2]
    slots = pick.shape[0] // seqs
    chunks = 4
    vmem = pl.BlockSpec(memory_space=pltpu.VMEM)
    anywhere = pl.BlockSpec(memory_space=pl.ANY)
    bf, f32 = jnp.bfloat16, jnp.float32
    dma = pltpu.SemaphoreType.DMA
    return pl.pallas_call(
        functools.partial(expert_kernel, seqs, heads, chunks),
        out_shape=jax.ShapeDtypeStruct((rows, width), bf),
        in_specs=[pl.BlockSpec(memory_space=pltpu.SMEM)] + [vmem] * 4 + [anywhere] * 3,
        out_specs=vmem,
        scratch_shapes=[
            pltpu.VMEM((width, hidden), bf),
            pltpu.VMEM((width, hidden), bf),
            pltpu.VMEM((hidden, width), bf),
            pltpu.VMEM((heads, rows, width), bf),
            pltpu.VMEM((seqs, slots, width), bf),
            pltpu.VMEM((seqs, slots, width), bf),
            pltpu.VMEM((seqs, slots, width), bf),
            pltpu.VMEM((seqs * slots, hidden), f32),
            pltpu.VMEM((seqs * slots, hidden), f32),
            pltpu.VMEM((seqs * slots, hidden), bf),
            pltpu.VMEM((heads, rows, width), f32),
            pltpu.VMEM((heads, rows, width), bf),
            pltpu.VMEM((heads, rows, width), bf),
            dma((3, chunks)),
            dma((chunks, heads)),
            dma((chunks, heads)),
            dma((chunks, seqs)),
            dma((chunks, seqs)),
            dma((chunks, seqs)),
            dma((chunks, seqs)),
            dma((chunks, heads)),
            dma((chunks, heads)),
            dma((2, chunks)),
        ],
        compiler_params=pltpu.CompilerParams(
            collective_id=0, has_side_effects=True, vmem_limit_bytes=60 * 1024 * 1024
        ),
    )(scales, normed, residual, pick, mix, gate, up, down)


def routing(expert_ids, expert_gates, seqs, heads):
    tok_rows = expert_ids.shape[0]
    capacity = 3 * tok_rows * TOPK // (2 * seqs * heads)
    slots = -(-capacity * heads // 16) * 16
    routed = jnp.concatenate([expert_ids.astype(jnp.float32), expert_gates], axis=1)
    routed = lax.all_gather(routed, "head", axis=0, tiled=True).T
    ids, gates = routed[:TOPK], routed[TOPK:]
    tokens = routed.shape[1]
    mine = (jnp.arange(seqs) * heads + lax.axis_index("head")).astype(jnp.float32)
    chosen = ids[None] == mine[:, None, None]
    hit = jnp.any(chosen, axis=1)
    weight = jnp.sum(jnp.where(chosen, gates[None], 0.0), axis=1)
    earlier = jnp.triu(jnp.ones((tokens, tokens), jnp.bfloat16), 1)
    rank = jnp.dot(hit.astype(jnp.bfloat16), earlier, preferred_element_type=jnp.float32)
    place = jnp.where(hit, rank, -1.0)
    slot = jnp.arange(slots, dtype=jnp.float32)
    taken = place[:, None, :] == slot[None, :, None]
    pick = taken.astype(jnp.bfloat16).reshape(seqs * slots, tokens)
    taken_t = place.T[:, :, None] == slot[None, None, :]
    mix = jnp.where(taken_t, weight.T[:, :, None], 0.0).astype(jnp.bfloat16)
    return pick, mix.reshape(tokens, seqs * slots)


def body(
    query,
    key,
    value,
    head_gain,
    out_weight,
    stream,
    model_gain,
    expert_ids,
    expert_gates,
    gate_weight,
    up_weight,
    down_weight,
    weight_scales,
):
    seqs, heads = lax.axis_size("seq"), lax.axis_size("head")
    pick, mix = routing(expert_ids, expert_gates, seqs, heads)
    seq_rows = query.shape[0]
    heads_local = head_gain.shape[0] // HD
    query_rows = query.reshape(seq_rows, heads_local, HD)
    key_rows = key.reshape(seq_rows, heads_local, HD)
    value_rows = value.reshape(seq_rows, heads_local, HD)
    scores = jnp.einsum("thd,shd->hts", query_rows, key_rows, preferred_element_type=jnp.float32)
    causal = jnp.tril(jnp.ones((seq_rows, seq_rows), dtype=bool))
    scores = jnp.where(causal[None, :, :], scores, 0.0).astype(jnp.bfloat16)
    local_part = jnp.einsum("hts,shd->thd", scores, value_rows, preferred_element_type=jnp.float32)
    block_state = jnp.einsum(
        "shd,she->hde", key_rows, value_rows, preferred_element_type=jnp.float32
    )
    position = lax.axis_index("seq")
    pieces = lax.all_gather(block_state[None], "seq", axis=0, tiled=True)
    piece_count = pieces.shape[0]
    selected = (jnp.arange(piece_count, dtype=jnp.int32) < position).astype(jnp.float32)
    prior_state = jnp.einsum("n,nhde->hde", selected, pieces)
    earlier_part = jnp.einsum(
        "thd,hde->the",
        query_rows,
        prior_state.astype(jnp.bfloat16),
        preferred_element_type=jnp.float32,
    )
    mixed_heads = local_part + earlier_part
    mean_square = jnp.mean(mixed_heads * mixed_heads, axis=-1, keepdims=True)
    head_normed = (
        mixed_heads * lax.rsqrt(mean_square + 1e-06) * head_gain.reshape(heads_local, HD)
    ).astype(jnp.bfloat16)
    head_normed = head_normed.reshape(seq_rows, heads_local * HD)
    full_out = lax.all_gather(out_weight, "seq", axis=1, tiled=True)
    attention = lax.psum_scatter(
        jnp.dot(head_normed, full_out, preferred_element_type=jnp.float32),
        "head",
        scatter_dimension=0,
        tiled=True,
    )
    residual = (stream.astype(jnp.float32) + attention).astype(jnp.bfloat16)
    residual_float = residual.astype(jnp.float32)
    mean_square = jnp.mean(residual_float * residual_float, axis=-1, keepdims=True)
    normed = (residual_float * lax.rsqrt(mean_square + 1e-06) * model_gain).astype(jnp.bfloat16)
    return experts_call(
        seqs,
        heads,
        weight_scales,
        normed,
        residual,
        pick,
        mix,
        gate_weight,
        up_weight,
        down_weight,
    )


def solution(mesh):
    return jax.shard_map(
        body,
        mesh=mesh,
        in_specs=(
            P("seq", "head"),
            P("seq", "head"),
            P("seq", "head"),
            P("head"),
            P("head", "seq"),
            P(("seq", "head"), None),
            P(),
            P(("seq", "head"), None),
            P(("seq", "head"), None),
            P(("seq", "head"), None, None),
            P(("seq", "head"), None, None),
            P(("seq", "head"), None, None),
            P(("seq", "head"), None),
        ),
        out_specs=P(("seq", "head"), None),
        check_vma=False,
    )
```

```python
import functools

import jax
import jax.numpy as jnp
from jax import lax
from jax.experimental import pallas as pl
from jax.experimental.pallas import tpu as pltpu
from jax.sharding import PartitionSpec as P

HD = 128
TOPK = 8
MESH = pl.DeviceIdType.MESH


def expert_kernel(
    seqs,
    heads,
    chunks,
    scale_ref,
    x_ref,
    res_ref,
    pick_ref,
    mix_ref,
    gate_hbm,
    up_hbm,
    down_hbm,
    out_ref,
    gate_v,
    up_v,
    down_v,
    gath,
    send,
    recv,
    back,
    acc_g,
    acc_u,
    act,
    part,
    psend,
    precv,
    wsem,
    zs,
    zr,
    ps,
    pr,
    rs,
    rr,
    cs,
    cr,
    lsem,
):
    s = lax.axis_index("seq")
    h = lax.axis_index("head")
    rows, width = x_ref.shape
    step = width // chunks
    slots = send.shape[1]
    block = heads * rows

    def cols(c):
        return pl.ds(pl.multiple_of(c * step, step), step)

    def plane(d):
        return lax.rem(s + d, seqs)

    def line(d):
        return lax.rem(h + d, heads)

    def weights(c):
        return (
            pltpu.make_async_copy(gate_hbm.at[0, cols(c), :], gate_v.at[cols(c), :], wsem.at[0, c]),
            pltpu.make_async_copy(up_hbm.at[0, cols(c), :], up_v.at[cols(c), :], wsem.at[1, c]),
            pltpu.make_async_copy(down_hbm.at[0, :, cols(c)], down_v.at[:, cols(c)], wsem.at[2, c]),
        )

    def remote(src, dst, ssem, rsem, seq, head):
        return pltpu.make_async_remote_copy(
            src_ref=src,
            dst_ref=dst,
            send_sem=ssem,
            recv_sem=rsem,
            device_id=(seq, head),
            device_id_type=MESH,
        )

    barrier = pltpu.get_barrier_semaphore()
    for d in range(1, seqs):
        pl.semaphore_signal(barrier, inc=1, device_id=(plane(d), h), device_id_type=MESH)
    for d in range(1, heads):
        pl.semaphore_signal(barrier, inc=1, device_id=(s, line(d)), device_id_type=MESH)

    def start_weights(c, carry):
        gate, up, _ = weights(c)
        gate.start()
        up.start()
        return carry

    def start_down(c, carry):
        weights(c)[2].start()
        return carry

    lax.fori_loop(0, chunks, start_weights, 0)
    lax.fori_loop(0, chunks, start_down, 0)
    gath[h] = x_ref[...]
    pl.semaphore_wait(barrier, seqs + heads - 2)

    def gather_copy(c, d, source, target):
        return remote(
            x_ref.at[:, cols(c)],
            gath.at[source, :, cols(c)],
            zs.at[c, d],
            zr.at[c, source],
            s,
            target,
        )

    def start_gather(c, carry):
        for d in range(1, heads):
            gather_copy(c, d, h, line(d)).start()
        return carry

    lax.fori_loop(0, chunks, start_gather, 0)

    def plane_copy(c, d):
        return remote(
            send.at[plane(d), :, cols(c)], recv.at[s, :, cols(c)], ps.at[c, d], pr.at[c, s],
            plane(d), h,
        )

    def plane_arrival(c, source):
        return remote(
            send.at[source, :, cols(c)], recv.at[source, :, cols(c)], ps.at[c, 0], pr.at[c, source],
            source, h,
        )

    def own_copy(c):
        return pltpu.make_async_copy(
            send.at[s, :, cols(c)], recv.at[s, :, cols(c)], lsem.at[0, c]
        )

    def pick(c):
        for d in range(1, heads):
            gather_copy(c, d, line(d), line(d)).wait_recv()
        picked = jnp.dot(
            pick_ref[...],
            gath[:, :, cols(c)].reshape(block, step),
            preferred_element_type=jnp.float32,
        )
        send[:, :, cols(c)] = picked.astype(jnp.bfloat16).reshape(seqs, slots, step)
        for d in range(1, seqs):
            plane_copy(c, d).start()
        own_copy(c).start()

    acc_g[...] = jnp.zeros_like(acc_g)
    acc_u[...] = jnp.zeros_like(acc_u)

    def expand(c):
        gate, up, _ = weights(c)
        gate.wait()
        up.wait()
        for d in range(1, seqs):
            plane_arrival(c, plane(d)).wait_recv()
        own_copy(c).wait()
        lhs = recv[:, :, cols(c)].reshape(seqs * slots, step)
        acc_g[...] += jnp.dot(lhs, gate_v[cols(c), :], preferred_element_type=jnp.float32)
        acc_u[...] += jnp.dot(lhs, up_v[cols(c), :], preferred_element_type=jnp.float32)

    pick(0)

    def forward(c, carry):
        pick(c)
        expand(c - 1)
        return carry

    lax.fori_loop(1, chunks, forward, 0)
    expand(chunks - 1)

    gate_scale = scale_ref[0, 0]
    up_scale = scale_ref[0, 1]
    down_scale = scale_ref[0, 2]

    def activate(i, carry):
        at = pl.ds(pl.multiple_of(i * slots, slots), slots)
        g = acc_g[at, :] * gate_scale
        act[at, :] = (g / (1.0 + jnp.exp(-g)) * (acc_u[at, :] * up_scale)).astype(jnp.bfloat16)
        return carry

    lax.fori_loop(0, seqs, activate, 0)

    def back_copy(c, d):
        return remote(
            recv.at[plane(d), :, cols(c)], back.at[s, :, cols(c)], rs.at[c, d], rr.at[c, s],
            plane(d), h,
        )

    def back_arrival(c, source):
        return remote(
            recv.at[source, :, cols(c)], back.at[source, :, cols(c)], rs.at[c, 0], rr.at[c, source],
            source, h,
        )

    def own_back(c):
        return pltpu.make_async_copy(
            recv.at[s, :, cols(c)], back.at[s, :, cols(c)], lsem.at[1, c]
        )

    def sum_copy(c, d):
        return remote(
            psend.at[line(d), :, cols(c)], precv.at[h, :, cols(c)], cs.at[c, d], cr.at[c, h],
            s, line(d),
        )

    def sum_arrival(c, source):
        return remote(
            psend.at[source, :, cols(c)], precv.at[source, :, cols(c)], cs.at[c, 0], cr.at[c, source],
            s, source,
        )

    def contract(c):
        weights(c)[2].wait()
        rows_out = jnp.dot(act[...], down_v[:, cols(c)], preferred_element_type=jnp.float32)
        recv[:, :, cols(c)] = (
            (rows_out * down_scale).astype(jnp.bfloat16).reshape(seqs, slots, step)
        )
        for d in range(1, seqs):
            back_copy(c, d).start()
        own_back(c).start()

    def combine(c):
        for d in range(1, seqs):
            back_arrival(c, plane(d)).wait_recv()
        own_back(c).wait()
        total = jnp.dot(
            mix_ref[...],
            back[:, :, cols(c)].reshape(seqs * slots, step),
            preferred_element_type=jnp.float32,
        ).reshape(heads, rows, step)
        part[:, :, cols(c)] = total
        psend[:, :, cols(c)] = total.astype(jnp.bfloat16)
        for d in range(1, heads):
            sum_copy(c, d).start()

    def finish(c):
        total = res_ref[:, cols(c)].astype(jnp.float32) + part[h, :, cols(c)]
        for d in range(1, heads):
            sum_arrival(c, line(d)).wait_recv()
            total = total + precv[line(d), :, cols(c)].astype(jnp.float32)
        out_ref[:, cols(c)] = total.astype(jnp.bfloat16)

    def run_contract(c, carry):
        contract(c)
        return carry

    def run_combine(c, carry):
        combine(c)
        return carry

    def run_finish(c, carry):
        finish(c)
        return carry

    def drain(c, carry):
        for d in range(1, heads):
            gather_copy(c, d, h, line(d)).wait_send()
            sum_copy(c, d).wait_send()
        for d in range(1, seqs):
            plane_copy(c, d).wait_send()
            back_copy(c, d).wait_send()
        return carry

    lax.fori_loop(0, chunks, run_contract, 0)
    lax.fori_loop(0, chunks, run_combine, 0)
    lax.fori_loop(0, chunks, run_finish, 0)
    lax.fori_loop(0, chunks, drain, 0)


def experts_call(seqs, heads, scales, normed, residual, pick, mix, gate, up, down):
    rows, width = normed.shape
    hidden = gate.shape[2]
    slots = pick.shape[0] // seqs
    chunks = 4
    vmem = pl.BlockSpec(memory_space=pltpu.VMEM)
    anywhere = pl.BlockSpec(memory_space=pl.ANY)
    bf, f32 = jnp.bfloat16, jnp.float32
    dma = pltpu.SemaphoreType.DMA
    return pl.pallas_call(
        functools.partial(expert_kernel, seqs, heads, chunks),
        out_shape=jax.ShapeDtypeStruct((rows, width), bf),
        in_specs=[pl.BlockSpec(memory_space=pltpu.SMEM)] + [vmem] * 4 + [anywhere] * 3,
        out_specs=vmem,
        scratch_shapes=[
            pltpu.VMEM((width, hidden), bf),
            pltpu.VMEM((width, hidden), bf),
            pltpu.VMEM((hidden, width), bf),
            pltpu.VMEM((heads, rows, width), bf),
            pltpu.VMEM((seqs, slots, width), bf),
            pltpu.VMEM((seqs, slots, width), bf),
            pltpu.VMEM((seqs, slots, width), bf),
            pltpu.VMEM((seqs * slots, hidden), f32),
            pltpu.VMEM((seqs * slots, hidden), f32),
            pltpu.VMEM((seqs * slots, hidden), bf),
            pltpu.VMEM((heads, rows, width), f32),
            pltpu.VMEM((heads, rows, width), bf),
            pltpu.VMEM((heads, rows, width), bf),
            dma((3, chunks)),
            dma((chunks, heads)),
            dma((chunks, heads)),
            dma((chunks, seqs)),
            dma((chunks, seqs)),
            dma((chunks, seqs)),
            dma((chunks, seqs)),
            dma((chunks, heads)),
            dma((chunks, heads)),
            dma((2, chunks)),
        ],
        compiler_params=pltpu.CompilerParams(
            collective_id=0, has_side_effects=True, vmem_limit_bytes=60 * 1024 * 1024
        ),
    )(scales, normed, residual, pick, mix, gate, up, down)


def attention_kernel(
    seqs,
    heads,
    halves,
    q_ref,
    k_ref,
    v_ref,
    gain_ref,
    w_hbm,
    stream_ref,
    model_ref,
    route_ref,
    res_ref,
    normed_ref,
    routes_ref,
    state,
    mixed,
    normed_heads,
    wbuf,
    own,
    psend,
    precv,
    routes,
    sds,
    sdr,
    sfs,
    sfr,
    wds,
    wdr,
    wfs,
    wfr,
    zs,
    zr,
    gs,
    gr,
    lsem,
):
    s = lax.axis_index("seq")
    h = lax.axis_index("head")
    tokens = q_ref.shape[0]
    rows, width = stream_ref.shape
    local = q_ref.shape[1] // HD
    block = w_hbm.shape[1]
    part = block // halves

    def flip(d):
        out, bit = s, 1
        while bit < seqs:
            if d & bit:
                out = out + bit * (1 - 2 * ((s // bit) % 2))
            bit *= 2
        return out

    partner = flip(1)

    def line(d):
        return lax.rem(h + d, heads)

    def remote(src, dst, ssem, rsem, seq, head):
        return pltpu.make_async_remote_copy(
            src_ref=src,
            dst_ref=dst,
            send_sem=ssem,
            recv_sem=rsem,
            device_id=(seq, head),
            device_id_type=MESH,
        )

    def state_direct(slot, peer):
        return remote(state.at[slot], state.at[slot], sds.at[peer], sdr.at[slot], peer, h)

    def state_pass(slot):
        return remote(state.at[slot], state.at[slot], sfs.at[slot], sfr.at[slot], partner, h)

    def w_at(slot, half):
        return wbuf.at[slot, :, pl.ds(half * part, part)]

    def w_direct(slot, half, peer):
        return remote(
            w_hbm.at[:, pl.ds(half * part, part)], w_at(slot, half),
            wds.at[peer, half], wdr.at[slot, half], peer, h,
        )

    def w_pass(slot, half):
        return remote(
            w_at(slot, half), w_at(slot, half), wfs.at[slot, half], wfr.at[slot, half], partner, h
        )

    def w_own_pass(half):
        return remote(
            w_hbm.at[:, pl.ds(half * part, part)], w_at(s, half),
            wfs.at[s, half], wfr.at[s, half], partner, h,
        )

    def w_own():
        return pltpu.make_async_copy(w_hbm, wbuf.at[s], lsem.at[0])

    def route_copy(slot, target):
        return remote(route_ref, routes.at[slot], gs.at[target], gr.at[slot], s, target)

    barrier = pltpu.get_barrier_semaphore()
    for d in range(1, seqs):
        pl.semaphore_signal(barrier, inc=1, device_id=(flip(d), h), device_id_type=MESH)
    for d in range(1, heads):
        pl.semaphore_signal(barrier, inc=1, device_id=(s, line(d)), device_id_type=MESH)
    w_own().start()
    routes[h] = route_ref[...]

    def lanes(i):
        return pl.ds(pl.multiple_of(i * HD, HD), HD)

    def block_state(i, carry):
        total = lax.dot_general(
            k_ref[:, lanes(i)], v_ref[:, lanes(i)], (((0,), (0,)), ((), ())),
            preferred_element_type=jnp.float32,
        )
        state[s, i] = total.astype(jnp.bfloat16)
        return carry

    lax.fori_loop(0, local, block_state, 0)
    pl.semaphore_wait(barrier, seqs + heads - 2)
    for d in range(2, seqs, 2):
        state_direct(s, flip(d)).start()
    state_pass(s).start()
    for d in range(1, heads):
        route_copy(h, line(d)).start()
    for half in range(halves):
        w_own_pass(half).start()
        for d in range(2, seqs, 2):
            w_direct(s, half, flip(d)).start()

    row = lax.broadcasted_iota(jnp.int32, (tokens, tokens), 0)
    col = lax.broadcasted_iota(jnp.int32, (tokens, tokens), 1)
    causal = col <= row

    def local_part(i, carry):
        scores = lax.dot_general(
            q_ref[:, lanes(i)], k_ref[:, lanes(i)], (((1,), (1,)), ((), ())),
            preferred_element_type=jnp.float32,
        )
        scores = jnp.where(causal, scores, 0.0).astype(jnp.bfloat16)
        mixed[:, lanes(i)] = jnp.dot(
            scores, v_ref[:, lanes(i)], preferred_element_type=jnp.float32
        )
        return carry

    lax.fori_loop(0, local, local_part, 0)

    for d in range(2, seqs, 2):
        state_direct(flip(d), flip(d)).wait_recv()
        state_pass(flip(d)).start()
    for d in range(1, seqs, 2):
        state_pass(flip(d)).wait_recv()

    def earlier_part(i, carry):
        prior = jnp.zeros((HD, HD), jnp.float32)
        for c in range(seqs):
            prior = prior + jnp.where(c < s, state[c, i].astype(jnp.float32), 0.0)
        total = mixed[:, lanes(i)] + jnp.dot(
            q_ref[:, lanes(i)], prior.astype(jnp.bfloat16), preferred_element_type=jnp.float32
        )
        mean_square = jnp.mean(total * total, axis=-1, keepdims=True)
        normed_heads[:, lanes(i)] = (
            total * lax.rsqrt(mean_square + 1e-06) * gain_ref[:, lanes(i)]
        ).astype(jnp.bfloat16)
        return carry

    lax.fori_loop(0, local, earlier_part, 0)

    def cols(slot, half):
        return pl.ds(pl.multiple_of(slot * block + half * part, part), part)

    def sum_copy(slot, half, d):
        return remote(
            psend.at[line(d), :, cols(slot, half)], precv.at[h, :, cols(slot, half)],
            zs.at[slot, half, d], zr.at[slot, half, h], s, line(d),
        )

    def sum_arrival(slot, half, source):
        return remote(
            psend.at[source, :, cols(slot, half)], precv.at[source, :, cols(slot, half)],
            zs.at[slot, half, 0], zr.at[slot, half, source], s, source,
        )

    def project(slot, half):
        total = jnp.dot(
            normed_heads[...],
            wbuf[slot, :, pl.ds(half * part, part)],
            preferred_element_type=jnp.float32,
        ).reshape(heads, rows, part)
        own[:, :, cols(slot, half)] = total
        psend[:, :, cols(slot, half)] = total.astype(jnp.bfloat16)
        for d in range(1, heads):
            sum_copy(slot, half, d).start()

    w_own().wait()
    for half in range(halves):
        for d in range(0, seqs, 2):
            if d:
                w_direct(flip(d), half, flip(d)).wait_recv()
                w_pass(flip(d), half).start()
            project(flip(d), half)
            w_pass(flip(d + 1), half).wait_recv()
            project(flip(d + 1), half)

    def settle(i, carry):
        for half in range(halves):
            for d in range(1, heads):
                sum_arrival(i, half, line(d)).wait_recv()
        return carry

    lax.fori_loop(0, seqs, settle, 0)
    for d in range(1, heads):
        route_copy(line(d), line(d)).wait_recv()
    routes_ref[...] = routes[...]

    group = 16

    def normalise(i, carry):
        at = pl.ds(pl.multiple_of(i * group, group), group)
        total = own[h, at, :]
        for d in range(1, heads):
            total = total + precv[line(d), at, :].astype(jnp.float32)
        residual = (stream_ref[at, :].astype(jnp.float32) + total).astype(jnp.bfloat16)
        res_ref[at, :] = residual
        value = residual.astype(jnp.float32)
        mean_square = jnp.mean(value * value, axis=-1, keepdims=True)
        normed_ref[at, :] = (
            value * lax.rsqrt(mean_square + 1e-06) * model_ref[...]
        ).astype(jnp.bfloat16)
        return carry

    lax.fori_loop(0, rows // group, normalise, 0)

    for d in range(2, seqs, 2):
        state_direct(s, flip(d)).wait_send()
        for half in range(halves):
            w_direct(s, half, flip(d)).wait_send()
    for d in range(0, seqs, 2):
        state_pass(flip(d)).wait_send()
        for half in range(halves):
            if d:
                w_pass(flip(d), half).wait_send()
            else:
                w_own_pass(half).wait_send()
    for d in range(1, heads):
        route_copy(h, line(d)).wait_send()

    def drain(i, carry):
        for half in range(halves):
            for d in range(1, heads):
                sum_copy(i, half, d).wait_send()
        return carry

    lax.fori_loop(0, seqs, drain, 0)


def attention_call(seqs, heads, query, key, value, gain, weight, stream, model_gain, route):
    tokens, features = query.shape
    rows, width = stream.shape
    local = features // HD
    block = weight.shape[1]
    halves = 2
    vmem = pl.BlockSpec(memory_space=pltpu.VMEM)
    anywhere = pl.BlockSpec(memory_space=pl.ANY)
    bf, f32 = jnp.bfloat16, jnp.float32
    dma = pltpu.SemaphoreType.DMA
    return pl.pallas_call(
        functools.partial(attention_kernel, seqs, heads, halves),
        out_shape=(
            jax.ShapeDtypeStruct((rows, width), bf),
            jax.ShapeDtypeStruct((rows, width), bf),
            jax.ShapeDtypeStruct((heads,) + route.shape, f32),
        ),
        in_specs=[vmem] * 4 + [anywhere] + [vmem] * 3,
        out_specs=(vmem,) * 3,
        scratch_shapes=[
            pltpu.VMEM((seqs, local, HD, HD), bf),
            pltpu.VMEM((tokens, features), f32),
            pltpu.VMEM((tokens, features), bf),
            pltpu.VMEM((seqs, features, block), bf),
            pltpu.VMEM((heads, rows, width), f32),
            pltpu.VMEM((heads, rows, width), bf),
            pltpu.VMEM((heads, rows, width), bf),
            pltpu.VMEM((heads,) + route.shape, f32),
            dma((seqs,)),
            dma((seqs,)),
            dma((seqs,)),
            dma((seqs,)),
            dma((seqs, halves)),
            dma((seqs, halves)),
            dma((seqs, halves)),
            dma((seqs, halves)),
            dma((seqs, halves, heads)),
            dma((seqs, halves, heads)),
            dma((heads,)),
            dma((heads,)),
            dma((1,)),
        ],
        compiler_params=pltpu.CompilerParams(
            collective_id=1, has_side_effects=True, vmem_limit_bytes=50000 * 1024
        ),
    )(
        query, key, value, gain.reshape(1, -1), weight, stream, model_gain.reshape(1, -1), route
    )


def routing(routed, seqs, heads):
    tok_rows = routed.shape[1]
    capacity = 3 * tok_rows * TOPK // (2 * seqs * heads)
    slots = -(-capacity * heads // 16) * 16
    routed = routed.reshape(-1, 2 * TOPK).T
    ids, gates = routed[:TOPK], routed[TOPK:]
    tokens = routed.shape[1]
    mine = (jnp.arange(seqs) * heads + lax.axis_index("head")).astype(jnp.float32)
    chosen = ids[None] == mine[:, None, None]
    hit = jnp.any(chosen, axis=1)
    weight = jnp.sum(jnp.where(chosen, gates[None], 0.0), axis=1)
    earlier = jnp.triu(jnp.ones((tokens, tokens), jnp.bfloat16), 1)
    rank = jnp.dot(hit.astype(jnp.bfloat16), earlier, preferred_element_type=jnp.float32)
    place = jnp.where(hit, rank, -1.0)
    slot = jnp.arange(slots, dtype=jnp.float32)
    taken = place[:, None, :] == slot[None, :, None]
    pick = taken.astype(jnp.bfloat16).reshape(seqs * slots, tokens)
    taken_t = place.T[:, :, None] == slot[None, None, :]
    mix = jnp.where(taken_t, weight.T[:, :, None], 0.0).astype(jnp.bfloat16)
    return pick, mix.reshape(tokens, seqs * slots)


def body(
    query,
    key,
    value,
    head_gain,
    out_weight,
    stream,
    model_gain,
    expert_ids,
    expert_gates,
    gate_weight,
    up_weight,
    down_weight,
    weight_scales,
):
    seqs, heads = lax.axis_size("seq"), lax.axis_size("head")
    route = jnp.concatenate([expert_ids.astype(jnp.float32), expert_gates], axis=1)
    residual, normed, routed = attention_call(
        seqs, heads, query, key, value, head_gain, out_weight, stream, model_gain, route
    )
    pick, mix = routing(routed, seqs, heads)
    return experts_call(
        seqs,
        heads,
        weight_scales,
        normed,
        residual,
        pick,
        mix,
        gate_weight,
        up_weight,
        down_weight,
    )


def solution(mesh):
    return jax.shard_map(
        body,
        mesh=mesh,
        in_specs=(
            P("seq", "head"),
            P("seq", "head"),
            P("seq", "head"),
            P("head"),
            P("head", "seq"),
            P(("seq", "head"), None),
            P(),
            P(("seq", "head"), None),
            P(("seq", "head"), None),
            P(("seq", "head"), None, None),
            P(("seq", "head"), None, None),
            P(("seq", "head"), None, None),
            P(("seq", "head"), None),
        ),
        out_specs=P(("seq", "head"), None),
        check_vma=False,
    )
```

```python
import functools

import jax
import jax.numpy as jnp
from jax import lax
from jax.experimental import pallas as pl
from jax.experimental.pallas import tpu as pltpu
from jax.sharding import PartitionSpec as P

HD = 128
TOPK = 8
MESH = pl.DeviceIdType.MESH


def expert_kernel(
    seqs,
    heads,
    chunks,
    scale_ref,
    x_ref,
    res_ref,
    pick_ref,
    mix_ref,
    gate_hbm,
    up_hbm,
    down_hbm,
    out_ref,
    gate_v,
    up_v,
    down_v,
    gath,
    send,
    recv,
    back,
    acc_g,
    acc_u,
    act,
    part,
    psend,
    precv,
    wsem,
    zs,
    zr,
    ps,
    pr,
    rs,
    rr,
    cs,
    cr,
    lsem,
):
    s = lax.axis_index("seq")
    h = lax.axis_index("head")
    rows, width = x_ref.shape
    step = width // chunks
    slots = send.shape[1]
    block = heads * rows

    def cols(c):
        return pl.ds(pl.multiple_of(c * step, step), step)

    def plane(d):
        return lax.rem(s + d, seqs)

    def line(d):
        return lax.rem(h + d, heads)

    def weights(c):
        return (
            pltpu.make_async_copy(gate_hbm.at[0, cols(c), :], gate_v.at[cols(c), :], wsem.at[0, c]),
            pltpu.make_async_copy(up_hbm.at[0, cols(c), :], up_v.at[cols(c), :], wsem.at[1, c]),
            pltpu.make_async_copy(down_hbm.at[0, :, cols(c)], down_v.at[:, cols(c)], wsem.at[2, c]),
        )

    def remote(src, dst, ssem, rsem, seq, head):
        return pltpu.make_async_remote_copy(
            src_ref=src,
            dst_ref=dst,
            send_sem=ssem,
            recv_sem=rsem,
            device_id=(seq, head),
            device_id_type=MESH,
        )

    barrier = pltpu.get_barrier_semaphore()
    for d in range(1, seqs):
        pl.semaphore_signal(barrier, inc=1, device_id=(plane(d), h), device_id_type=MESH)
    for d in range(1, heads):
        pl.semaphore_signal(barrier, inc=1, device_id=(s, line(d)), device_id_type=MESH)

    def start_weights(c, carry):
        gate, up, _ = weights(c)
        gate.start()
        up.start()
        return carry

    def start_down(c, carry):
        weights(c)[2].start()
        return carry

    lax.fori_loop(0, chunks, start_weights, 0)
    lax.fori_loop(0, chunks, start_down, 0)
    gath[h] = x_ref[...]
    pl.semaphore_wait(barrier, seqs + heads - 2)

    def gather_copy(c, d, source, target):
        return remote(
            x_ref.at[:, cols(c)],
            gath.at[source, :, cols(c)],
            zs.at[c, d],
            zr.at[c, source],
            s,
            target,
        )

    def start_gather(c, carry):
        for d in range(1, heads):
            gather_copy(c, d, h, line(d)).start()
        return carry

    lax.fori_loop(0, chunks, start_gather, 0)

    def plane_copy(c, d):
        return remote(
            send.at[plane(d), :, cols(c)], recv.at[s, :, cols(c)], ps.at[c, d], pr.at[c, s],
            plane(d), h,
        )

    def plane_arrival(c, source):
        return remote(
            send.at[source, :, cols(c)], recv.at[source, :, cols(c)], ps.at[c, 0], pr.at[c, source],
            source, h,
        )

    def own_copy(c):
        return pltpu.make_async_copy(
            send.at[s, :, cols(c)], recv.at[s, :, cols(c)], lsem.at[0, c]
        )

    def pick(c):
        for d in range(1, heads):
            gather_copy(c, d, line(d), line(d)).wait_recv()
        picked = jnp.dot(
            pick_ref[...],
            gath[:, :, cols(c)].reshape(block, step),
            preferred_element_type=jnp.float32,
        )
        send[:, :, cols(c)] = picked.astype(jnp.bfloat16).reshape(seqs, slots, step)
        for d in range(1, seqs):
            plane_copy(c, d).start()
        own_copy(c).start()

    acc_g[...] = jnp.zeros_like(acc_g)
    acc_u[...] = jnp.zeros_like(acc_u)

    def expand(c):
        gate, up, _ = weights(c)
        gate.wait()
        up.wait()
        for d in range(1, seqs):
            plane_arrival(c, plane(d)).wait_recv()
        own_copy(c).wait()
        lhs = recv[:, :, cols(c)].reshape(seqs * slots, step)
        acc_g[...] += jnp.dot(lhs, gate_v[cols(c), :], preferred_element_type=jnp.float32)
        acc_u[...] += jnp.dot(lhs, up_v[cols(c), :], preferred_element_type=jnp.float32)

    pick(0)

    def forward(c, carry):
        pick(c)
        expand(c - 1)
        return carry

    lax.fori_loop(1, chunks, forward, 0)
    expand(chunks - 1)

    gate_scale = scale_ref[0, 0]
    up_scale = scale_ref[0, 1]
    down_scale = scale_ref[0, 2]

    def activate(i, carry):
        at = pl.ds(pl.multiple_of(i * slots, slots), slots)
        g = acc_g[at, :] * gate_scale
        act[at, :] = (g / (1.0 + jnp.exp(-g)) * (acc_u[at, :] * up_scale)).astype(jnp.bfloat16)
        return carry

    lax.fori_loop(0, seqs, activate, 0)

    def back_copy(c, d):
        return remote(
            recv.at[plane(d), :, cols(c)], back.at[s, :, cols(c)], rs.at[c, d], rr.at[c, s],
            plane(d), h,
        )

    def back_arrival(c, source):
        return remote(
            recv.at[source, :, cols(c)], back.at[source, :, cols(c)], rs.at[c, 0], rr.at[c, source],
            source, h,
        )

    def own_back(c):
        return pltpu.make_async_copy(
            recv.at[s, :, cols(c)], back.at[s, :, cols(c)], lsem.at[1, c]
        )

    def sum_copy(c, d):
        return remote(
            psend.at[line(d), :, cols(c)], precv.at[h, :, cols(c)], cs.at[c, d], cr.at[c, h],
            s, line(d),
        )

    def sum_arrival(c, source):
        return remote(
            psend.at[source, :, cols(c)], precv.at[source, :, cols(c)], cs.at[c, 0], cr.at[c, source],
            s, source,
        )

    def contract(c):
        weights(c)[2].wait()
        rows_out = jnp.dot(act[...], down_v[:, cols(c)], preferred_element_type=jnp.float32)
        recv[:, :, cols(c)] = (
            (rows_out * down_scale).astype(jnp.bfloat16).reshape(seqs, slots, step)
        )
        for d in range(1, seqs):
            back_copy(c, d).start()
        own_back(c).start()

    def combine(c):
        for d in range(1, seqs):
            back_arrival(c, plane(d)).wait_recv()
        own_back(c).wait()
        total = jnp.dot(
            mix_ref[...],
            back[:, :, cols(c)].reshape(seqs * slots, step),
            preferred_element_type=jnp.float32,
        ).reshape(heads, rows, step)
        part[:, :, cols(c)] = total
        psend[:, :, cols(c)] = total.astype(jnp.bfloat16)
        for d in range(1, heads):
            sum_copy(c, d).start()

    def finish(c):
        total = res_ref[:, cols(c)].astype(jnp.float32) + part[h, :, cols(c)]
        for d in range(1, heads):
            sum_arrival(c, line(d)).wait_recv()
            total = total + precv[line(d), :, cols(c)].astype(jnp.float32)
        out_ref[:, cols(c)] = total.astype(jnp.bfloat16)

    def run_contract(c, carry):
        contract(c)
        return carry

    def run_combine(c, carry):
        combine(c)
        return carry

    def run_finish(c, carry):
        finish(c)
        return carry

    def drain(c, carry):
        for d in range(1, heads):
            gather_copy(c, d, h, line(d)).wait_send()
            sum_copy(c, d).wait_send()
        for d in range(1, seqs):
            plane_copy(c, d).wait_send()
            back_copy(c, d).wait_send()
        return carry

    lax.fori_loop(0, chunks, run_contract, 0)
    lax.fori_loop(0, chunks, run_combine, 0)
    lax.fori_loop(0, chunks, run_finish, 0)
    lax.fori_loop(0, chunks, drain, 0)


def experts_call(seqs, heads, scales, normed, residual, pick, mix, gate, up, down):
    rows, width = normed.shape
    hidden = gate.shape[2]
    slots = pick.shape[0] // seqs
    chunks = 8
    vmem = pl.BlockSpec(memory_space=pltpu.VMEM)
    anywhere = pl.BlockSpec(memory_space=pl.ANY)
    bf, f32 = jnp.bfloat16, jnp.float32
    dma = pltpu.SemaphoreType.DMA
    return pl.pallas_call(
        functools.partial(expert_kernel, seqs, heads, chunks),
        out_shape=jax.ShapeDtypeStruct((rows, width), bf),
        in_specs=[pl.BlockSpec(memory_space=pltpu.SMEM)] + [vmem] * 4 + [anywhere] * 3,
        out_specs=vmem,
        scratch_shapes=[
            pltpu.VMEM((width, hidden), bf),
            pltpu.VMEM((width, hidden), bf),
            pltpu.VMEM((hidden, width), bf),
            pltpu.VMEM((heads, rows, width), bf),
            pltpu.VMEM((seqs, slots, width), bf),
            pltpu.VMEM((seqs, slots, width), bf),
            pltpu.VMEM((seqs, slots, width), bf),
            pltpu.VMEM((seqs * slots, hidden), f32),
            pltpu.VMEM((seqs * slots, hidden), f32),
            pltpu.VMEM((seqs * slots, hidden), bf),
            pltpu.VMEM((heads, rows, width), f32),
            pltpu.VMEM((heads, rows, width), bf),
            pltpu.VMEM((heads, rows, width), bf),
            dma((3, chunks)),
            dma((chunks, heads)),
            dma((chunks, heads)),
            dma((chunks, seqs)),
            dma((chunks, seqs)),
            dma((chunks, seqs)),
            dma((chunks, seqs)),
            dma((chunks, heads)),
            dma((chunks, heads)),
            dma((2, chunks)),
        ],
        compiler_params=pltpu.CompilerParams(
            collective_id=0, has_side_effects=True, vmem_limit_bytes=60 * 1024 * 1024
        ),
    )(scales, normed, residual, pick, mix, gate, up, down)


def attention_kernel(
    seqs,
    heads,
    halves,
    q_hbm,
    k_hbm,
    v_hbm,
    gain_ref,
    w_hbm,
    stream_hbm,
    model_ref,
    route_ref,
    res_ref,
    normed_ref,
    routes_ref,
    q_ref,
    k_ref,
    v_ref,
    stream_ref,
    state,
    mixed,
    normed_heads,
    wbuf,
    own,
    psend,
    precv,
    routes,
    sds,
    sdr,
    sfs,
    sfr,
    wds,
    wdr,
    wfs,
    wfr,
    zs,
    zr,
    gs,
    gr,
    lsem,
):
    s = lax.axis_index("seq")
    h = lax.axis_index("head")
    tokens = q_ref.shape[0]
    rows, width = stream_ref.shape
    bits = [2**i for i in range(1, seqs.bit_length() - 1)]
    orders = [bits, bits[::-1]]
    local = q_ref.shape[1] // HD
    block = w_hbm.shape[1]
    part = block // halves

    def flip(d):
        out, bit = s, 1
        while bit < seqs:
            if d & bit:
                out = out + bit * (1 - 2 * ((s // bit) % 2))
            bit *= 2
        return out

    partner = flip(1)

    def line(d):
        return lax.rem(h + d, heads)

    def remote(src, dst, ssem, rsem, seq, head):
        return pltpu.make_async_remote_copy(
            src_ref=src,
            dst_ref=dst,
            send_sem=ssem,
            recv_sem=rsem,
            device_id=(seq, head),
            device_id_type=MESH,
        )

    def state_direct(slot, peer):
        return remote(state.at[slot], state.at[slot], sds.at[peer], sdr.at[slot], peer, h)

    def state_pass(slot):
        return remote(state.at[slot], state.at[slot], sfs.at[slot], sfr.at[slot], partner, h)

    def w_at(slot, half):
        return wbuf.at[slot, :, pl.ds(half * part, part)]

    def w_first(half, bit):
        return remote(
            w_hbm.at[:, pl.ds(half * part, part)], w_at(s, half),
            wds.at[s, half, bits.index(bit)], wdr.at[s, half], flip(bit), h,
        )

    def w_relay(slot, half, bit):
        return remote(
            w_at(slot, half), w_at(slot, half),
            wds.at[slot, half, bits.index(bit)], wdr.at[slot, half], flip(bit), h,
        )

    def later_bits(d, half):
        order = orders[half]
        last = max(order.index(bit) for bit in bits if d & bit)
        return order[last + 1 :]

    def w_pass(slot, half):
        return remote(
            w_at(slot, half), w_at(slot, half), wfs.at[slot, half], wfr.at[slot, half], partner, h
        )

    def w_own_pass(half):
        return remote(
            w_hbm.at[:, pl.ds(half * part, part)], w_at(s, half),
            wfs.at[s, half], wfr.at[s, half], partner, h,
        )

    def w_own():
        return pltpu.make_async_copy(w_hbm, wbuf.at[s], lsem.at[0])

    def route_copy(slot, target):
        return remote(route_ref, routes.at[slot], gs.at[target], gr.at[slot], s, target)

    barrier = pltpu.get_barrier_semaphore()
    for d in range(1, seqs):
        pl.semaphore_signal(barrier, inc=1, device_id=(flip(d), h), device_id_type=MESH)
    for d in range(1, heads):
        pl.semaphore_signal(barrier, inc=1, device_id=(s, line(d)), device_id_type=MESH)
    loads = [
        pltpu.make_async_copy(source, target, lsem.at[1 + i])
        for i, (source, target) in enumerate(
            [(k_hbm, k_ref), (v_hbm, v_ref), (q_hbm, q_ref), (stream_hbm, stream_ref)]
        )
    ]
    for load in loads:
        load.start()
    w_own().start()
    routes[h] = route_ref[...]
    loads[0].wait()
    loads[1].wait()

    def lanes(i):
        return pl.ds(pl.multiple_of(i * HD, HD), HD)

    def block_state(i, carry):
        total = lax.dot_general(
            k_ref[:, lanes(i)], v_ref[:, lanes(i)], (((0,), (0,)), ((), ())),
            preferred_element_type=jnp.float32,
        )
        state[s, i] = total.astype(jnp.bfloat16)
        return carry

    lax.fori_loop(0, local, block_state, 0)
    pl.semaphore_wait(barrier, seqs + heads - 2)
    for d in range(2, seqs, 2):
        state_direct(s, flip(d)).start()
    state_pass(s).start()
    for d in range(1, heads):
        route_copy(h, line(d)).start()
    for i in range(len(bits)):
        for half in range(halves):
            w_first(half, orders[half][i]).start()
    for half in range(halves):
        w_own_pass(half).start()
    loads[2].wait()

    row = lax.broadcasted_iota(jnp.int32, (tokens, tokens), 0)
    col = lax.broadcasted_iota(jnp.int32, (tokens, tokens), 1)
    causal = col <= row

    def local_part(i, carry):
        scores = lax.dot_general(
            q_ref[:, lanes(i)], k_ref[:, lanes(i)], (((1,), (1,)), ((), ())),
            preferred_element_type=jnp.float32,
        )
        scores = jnp.where(causal, scores, 0.0).astype(jnp.bfloat16)
        mixed[:, lanes(i)] = jnp.dot(
            scores, v_ref[:, lanes(i)], preferred_element_type=jnp.float32
        )
        return carry

    lax.fori_loop(0, local, local_part, 0)

    for d in range(2, seqs, 2):
        state_direct(flip(d), flip(d)).wait_recv()
        state_pass(flip(d)).start()
    for d in range(1, seqs, 2):
        state_pass(flip(d)).wait_recv()

    def earlier_part(i, carry):
        prior = jnp.zeros((HD, HD), jnp.float32)
        for c in range(seqs):
            prior = prior + jnp.where(c < s, state[c, i].astype(jnp.float32), 0.0)
        total = mixed[:, lanes(i)] + jnp.dot(
            q_ref[:, lanes(i)], prior.astype(jnp.bfloat16), preferred_element_type=jnp.float32
        )
        mean_square = jnp.mean(total * total, axis=-1, keepdims=True)
        normed_heads[:, lanes(i)] = (
            total * lax.rsqrt(mean_square + 1e-06) * gain_ref[:, lanes(i)]
        ).astype(jnp.bfloat16)
        return carry

    lax.fori_loop(0, local, earlier_part, 0)

    def cols(slot, half):
        return pl.ds(pl.multiple_of(slot * block + half * part, part), part)

    def sum_copy(slot, half, d):
        return remote(
            psend.at[line(d), :, cols(slot, half)], precv.at[h, :, cols(slot, half)],
            zs.at[slot, half, d], zr.at[slot, half, h], s, line(d),
        )

    def sum_arrival(slot, half, source):
        return remote(
            psend.at[source, :, cols(slot, half)], precv.at[source, :, cols(slot, half)],
            zs.at[slot, half, 0], zr.at[slot, half, source], s, source,
        )

    def project(slot, half):
        total = jnp.dot(
            normed_heads[...],
            wbuf[slot, :, pl.ds(half * part, part)],
            preferred_element_type=jnp.float32,
        ).reshape(heads, rows, part)
        own[:, :, cols(slot, half)] = total
        psend[:, :, cols(slot, half)] = total.astype(jnp.bfloat16)
        for d in range(1, heads):
            sum_copy(slot, half, d).start()

    w_own().wait()
    evens = list(range(0, seqs, 2))
    schedule = []
    for low, high in zip(
        sorted(evens, key=lambda d: (d.bit_count(), d)),
        sorted(evens, key=lambda d: (d.bit_count(), -d)),
    ):
        schedule += [(low, 0), (high, 1)]
    for i in range(0, len(schedule), 2):
        pair = schedule[i : i + 2]
        for d, half in pair:
            if d:
                w_relay(flip(d), half, bits[0]).wait_recv()
                for bit in later_bits(d, half):
                    w_relay(flip(d), half, bit).start()
                w_pass(flip(d), half).start()
        for d, half in pair:
            project(flip(d), half)
        for d, half in pair:
            w_pass(flip(d + 1), half).wait_recv()
            project(flip(d + 1), half)

    def settle(i, carry):
        for half in range(halves):
            for d in range(1, heads):
                sum_arrival(i, half, line(d)).wait_recv()
        return carry

    lax.fori_loop(0, seqs, settle, 0)
    for d in range(1, heads):
        route_copy(line(d), line(d)).wait_recv()
    routes_ref[...] = routes[...]

    loads[3].wait()
    group = 16

    def normalise(i, carry):
        at = pl.ds(pl.multiple_of(i * group, group), group)
        total = own[h, at, :]
        for d in range(1, heads):
            total = total + precv[line(d), at, :].astype(jnp.float32)
        residual = (stream_ref[at, :].astype(jnp.float32) + total).astype(jnp.bfloat16)
        res_ref[at, :] = residual
        value = residual.astype(jnp.float32)
        mean_square = jnp.mean(value * value, axis=-1, keepdims=True)
        normed_ref[at, :] = (
            value * lax.rsqrt(mean_square + 1e-06) * model_ref[...]
        ).astype(jnp.bfloat16)
        return carry

    lax.fori_loop(0, rows // group, normalise, 0)

    for d in range(2, seqs, 2):
        state_direct(s, flip(d)).wait_send()
        for half in range(halves):
            for bit in later_bits(d, half):
                w_relay(flip(d), half, bit).wait_send()
    for half in range(halves):
        for bit in bits:
            w_first(half, bit).wait_send()
    for d in range(0, seqs, 2):
        state_pass(flip(d)).wait_send()
        for half in range(halves):
            if d:
                w_pass(flip(d), half).wait_send()
            else:
                w_own_pass(half).wait_send()
    for d in range(1, heads):
        route_copy(h, line(d)).wait_send()

    def drain(i, carry):
        for half in range(halves):
            for d in range(1, heads):
                sum_copy(i, half, d).wait_send()
        return carry

    lax.fori_loop(0, seqs, drain, 0)


def attention_call(seqs, heads, query, key, value, gain, weight, stream, model_gain, route):
    tokens, features = query.shape
    rows, width = stream.shape
    local = features // HD
    block = weight.shape[1]
    halves = 2
    vmem = pl.BlockSpec(memory_space=pltpu.VMEM)
    anywhere = pl.BlockSpec(memory_space=pl.ANY)
    bf, f32 = jnp.bfloat16, jnp.float32
    dma = pltpu.SemaphoreType.DMA
    return pl.pallas_call(
        functools.partial(attention_kernel, seqs, heads, halves),
        out_shape=(
            jax.ShapeDtypeStruct((rows, width), bf),
            jax.ShapeDtypeStruct((rows, width), bf),
            jax.ShapeDtypeStruct((heads,) + route.shape, f32),
        ),
        in_specs=[anywhere] * 3 + [vmem] + [anywhere] * 2 + [vmem] * 2,
        out_specs=(vmem,) * 3,
        scratch_shapes=[
            pltpu.VMEM((tokens, features), bf),
            pltpu.VMEM((tokens, features), bf),
            pltpu.VMEM((tokens, features), bf),
            pltpu.VMEM((rows, width), bf),
            pltpu.VMEM((seqs, local, HD, HD), bf),
            pltpu.VMEM((tokens, features), f32),
            pltpu.VMEM((tokens, features), bf),
            pltpu.VMEM((seqs, features, block), bf),
            pltpu.VMEM((heads, rows, width), f32),
            pltpu.VMEM((heads, rows, width), bf),
            pltpu.VMEM((heads, rows, width), bf),
            pltpu.VMEM((heads,) + route.shape, f32),
            dma((seqs,)),
            dma((seqs,)),
            dma((seqs,)),
            dma((seqs,)),
            dma((seqs, halves, seqs.bit_length())),
            dma((seqs, halves)),
            dma((seqs, halves)),
            dma((seqs, halves)),
            dma((seqs, halves, heads)),
            dma((seqs, halves, heads)),
            dma((heads,)),
            dma((heads,)),
            dma((5,)),
        ],
        compiler_params=pltpu.CompilerParams(
            collective_id=1, has_side_effects=True, vmem_limit_bytes=60 * 1024 * 1024
        ),
    )(
        query, key, value, gain.reshape(1, -1), weight, stream, model_gain.reshape(1, -1), route
    )


def routing(routed, seqs, heads):
    tok_rows = routed.shape[1]
    capacity = 3 * tok_rows * TOPK // (2 * seqs * heads)
    slots = -(-capacity * heads // 16) * 16
    routed = routed.reshape(-1, 2 * TOPK).T
    ids, gates = routed[:TOPK], routed[TOPK:]
    tokens = routed.shape[1]
    mine = (jnp.arange(seqs) * heads + lax.axis_index("head")).astype(jnp.float32)
    chosen = ids[None] == mine[:, None, None]
    hit = jnp.any(chosen, axis=1)
    weight = jnp.sum(jnp.where(chosen, gates[None], 0.0), axis=1)
    earlier = jnp.triu(jnp.ones((tokens, tokens), jnp.bfloat16), 1)
    rank = jnp.dot(hit.astype(jnp.bfloat16), earlier, preferred_element_type=jnp.float32)
    place = jnp.where(hit, rank, -1.0)
    slot = jnp.arange(slots, dtype=jnp.float32)
    taken = place[:, None, :] == slot[None, :, None]
    pick = taken.astype(jnp.bfloat16).reshape(seqs * slots, tokens)
    taken_t = place.T[:, :, None] == slot[None, None, :]
    mix = jnp.where(taken_t, weight.T[:, :, None], 0.0).astype(jnp.bfloat16)
    return pick, mix.reshape(tokens, seqs * slots)


def body(
    query,
    key,
    value,
    head_gain,
    out_weight,
    stream,
    model_gain,
    expert_ids,
    expert_gates,
    gate_weight,
    up_weight,
    down_weight,
    weight_scales,
):
    seqs, heads = lax.axis_size("seq"), lax.axis_size("head")
    route = jnp.concatenate([expert_ids.astype(jnp.float32), expert_gates], axis=1)
    residual, normed, routed = attention_call(
        seqs, heads, query, key, value, head_gain, out_weight, stream, model_gain, route
    )
    pick, mix = routing(routed, seqs, heads)
    return experts_call(
        seqs,
        heads,
        weight_scales,
        normed,
        residual,
        pick,
        mix,
        gate_weight,
        up_weight,
        down_weight,
    )


def solution(mesh):
    return jax.shard_map(
        body,
        mesh=mesh,
        in_specs=(
            P("seq", "head"),
            P("seq", "head"),
            P("seq", "head"),
            P("head"),
            P("head", "seq"),
            P(("seq", "head"), None),
            P(),
            P(("seq", "head"), None),
            P(("seq", "head"), None),
            P(("seq", "head"), None, None),
            P(("seq", "head"), None, None),
            P(("seq", "head"), None, None),
            P(("seq", "head"), None),
        ),
        out_specs=P(("seq", "head"), None),
        check_vma=False,
    )
```

```python
import functools

import jax
import jax.numpy as jnp
from jax import lax
from jax.experimental import pallas as pl
from jax.experimental.pallas import tpu as pltpu
from jax.sharding import PartitionSpec as P

HD = 128
TOPK = 8
MESH = pl.DeviceIdType.MESH


def expert_kernel(
    seqs,
    heads,
    chunks,
    scale_ref,
    x_ref,
    res_ref,
    pick_ref,
    mix_ref,
    gate_hbm,
    up_hbm,
    down_hbm,
    out_ref,
    gate_v,
    up_v,
    down_v,
    gath,
    send,
    recv,
    back,
    acc_g,
    acc_u,
    act,
    part,
    psend,
    precv,
    wsem,
    zs,
    zr,
    ps,
    pr,
    rs,
    rr,
    cs,
    cr,
    lsem,
):
    s = lax.axis_index("seq")
    h = lax.axis_index("head")
    rows, width = x_ref.shape
    step = width // chunks
    slots = send.shape[1]
    block = heads * rows

    def cols(c):
        return pl.ds(pl.multiple_of(c * step, step), step)

    def plane(d):
        return lax.rem(s + d, seqs)

    def line(d):
        return lax.rem(h + d, heads)

    def weights(c):
        return (
            pltpu.make_async_copy(gate_hbm.at[0, cols(c), :], gate_v.at[cols(c), :], wsem.at[0, c]),
            pltpu.make_async_copy(up_hbm.at[0, cols(c), :], up_v.at[cols(c), :], wsem.at[1, c]),
            pltpu.make_async_copy(down_hbm.at[0, :, cols(c)], down_v.at[:, cols(c)], wsem.at[2, c]),
        )

    def remote(src, dst, ssem, rsem, seq, head):
        return pltpu.make_async_remote_copy(
            src_ref=src,
            dst_ref=dst,
            send_sem=ssem,
            recv_sem=rsem,
            device_id=(seq, head),
            device_id_type=MESH,
        )

    barrier = pltpu.get_barrier_semaphore()
    for d in range(1, seqs):
        pl.semaphore_signal(barrier, inc=1, device_id=(plane(d), h), device_id_type=MESH)
    for d in range(1, heads):
        pl.semaphore_signal(barrier, inc=1, device_id=(s, line(d)), device_id_type=MESH)

    def start_weights(c, carry):
        gate, up, _ = weights(c)
        gate.start()
        up.start()
        return carry

    def start_down(c, carry):
        weights(c)[2].start()
        return carry

    lax.fori_loop(0, chunks, start_weights, 0)
    lax.fori_loop(0, chunks, start_down, 0)
    gath[h] = x_ref[...]
    pl.semaphore_wait(barrier, seqs + heads - 2)

    def gather_copy(c, d, source, target):
        return remote(
            x_ref.at[:, cols(c)],
            gath.at[source, :, cols(c)],
            zs.at[c, d],
            zr.at[c, source],
            s,
            target,
        )

    def start_gather(c, carry):
        for d in range(1, heads):
            gather_copy(c, d, h, line(d)).start()
        return carry

    lax.fori_loop(0, chunks, start_gather, 0)

    def plane_copy(c, d):
        return remote(
            send.at[plane(d), :, cols(c)], recv.at[s, :, cols(c)], ps.at[c, d], pr.at[c, s],
            plane(d), h,
        )

    def plane_arrival(c, source):
        return remote(
            send.at[source, :, cols(c)], recv.at[source, :, cols(c)], ps.at[c, 0], pr.at[c, source],
            source, h,
        )

    def own_copy(c):
        return pltpu.make_async_copy(
            send.at[s, :, cols(c)], recv.at[s, :, cols(c)], lsem.at[0, c]
        )

    def pick(c):
        for d in range(1, heads):
            gather_copy(c, d, line(d), line(d)).wait_recv()
        picked = jnp.dot(
            pick_ref[...],
            gath[:, :, cols(c)].reshape(block, step),
            preferred_element_type=jnp.float32,
        )
        send[:, :, cols(c)] = picked.astype(jnp.bfloat16).reshape(seqs, slots, step)
        for d in range(1, seqs):
            plane_copy(c, d).start()
        own_copy(c).start()

    acc_g[...] = jnp.zeros_like(acc_g)
    acc_u[...] = jnp.zeros_like(acc_u)

    def expand(c):
        gate, up, _ = weights(c)
        gate.wait()
        up.wait()
        for d in range(1, seqs):
            plane_arrival(c, plane(d)).wait_recv()
        own_copy(c).wait()
        lhs = recv[:, :, cols(c)].reshape(seqs * slots, step)
        acc_g[...] += jnp.dot(lhs, gate_v[cols(c), :], preferred_element_type=jnp.float32)
        acc_u[...] += jnp.dot(lhs, up_v[cols(c), :], preferred_element_type=jnp.float32)

    pick(0)

    def forward(c, carry):
        pick(c)
        expand(c - 1)
        return carry

    lax.fori_loop(1, chunks, forward, 0)
    expand(chunks - 1)

    gate_scale = scale_ref[0, 0]
    up_scale = scale_ref[0, 1]
    down_scale = scale_ref[0, 2]

    def activate(i, carry):
        at = pl.ds(pl.multiple_of(i * slots, slots), slots)
        g = acc_g[at, :] * gate_scale
        act[at, :] = (g / (1.0 + jnp.exp(-g)) * (acc_u[at, :] * up_scale)).astype(jnp.bfloat16)
        return carry

    lax.fori_loop(0, seqs, activate, 0)

    def back_copy(c, d):
        return remote(
            recv.at[plane(d), :, cols(c)], back.at[s, :, cols(c)], rs.at[c, d], rr.at[c, s],
            plane(d), h,
        )

    def back_arrival(c, source):
        return remote(
            recv.at[source, :, cols(c)], back.at[source, :, cols(c)], rs.at[c, 0], rr.at[c, source],
            source, h,
        )

    def own_back(c):
        return pltpu.make_async_copy(
            recv.at[s, :, cols(c)], back.at[s, :, cols(c)], lsem.at[1, c]
        )

    def sum_copy(c, d):
        return remote(
            psend.at[line(d), :, cols(c)], precv.at[h, :, cols(c)], cs.at[c, d], cr.at[c, h],
            s, line(d),
        )

    def sum_arrival(c, source):
        return remote(
            psend.at[source, :, cols(c)], precv.at[source, :, cols(c)], cs.at[c, 0], cr.at[c, source],
            s, source,
        )

    def contract(c):
        weights(c)[2].wait()
        rows_out = jnp.dot(act[...], down_v[:, cols(c)], preferred_element_type=jnp.float32)
        recv[:, :, cols(c)] = (
            (rows_out * down_scale).astype(jnp.bfloat16).reshape(seqs, slots, step)
        )
        for d in range(1, seqs):
            back_copy(c, d).start()
        own_back(c).start()

    def combine(c):
        for d in range(1, seqs):
            back_arrival(c, plane(d)).wait_recv()
        own_back(c).wait()
        total = jnp.dot(
            mix_ref[...],
            back[:, :, cols(c)].reshape(seqs * slots, step),
            preferred_element_type=jnp.float32,
        ).reshape(heads, rows, step)
        part[:, :, cols(c)] = total
        psend[:, :, cols(c)] = total.astype(jnp.bfloat16)
        for d in range(1, heads):
            sum_copy(c, d).start()

    def finish(c):
        total = res_ref[:, cols(c)].astype(jnp.float32) + part[h, :, cols(c)]
        for d in range(1, heads):
            sum_arrival(c, line(d)).wait_recv()
            total = total + precv[line(d), :, cols(c)].astype(jnp.float32)
        out_ref[:, cols(c)] = total.astype(jnp.bfloat16)

    def run_contract(c, carry):
        contract(c)
        return carry

    def run_combine(c, carry):
        combine(c)
        return carry

    def run_finish(c, carry):
        finish(c)
        return carry

    def drain(c, carry):
        for d in range(1, heads):
            gather_copy(c, d, h, line(d)).wait_send()
            sum_copy(c, d).wait_send()
        for d in range(1, seqs):
            plane_copy(c, d).wait_send()
            back_copy(c, d).wait_send()
        return carry

    lax.fori_loop(0, chunks, run_contract, 0)
    lax.fori_loop(0, chunks, run_combine, 0)
    lax.fori_loop(0, chunks, run_finish, 0)
    lax.fori_loop(0, chunks, drain, 0)


def experts_call(seqs, heads, scales, normed, residual, pick, mix, gate, up, down):
    rows, width = normed.shape
    hidden = gate.shape[2]
    slots = pick.shape[0] // seqs
    chunks = 16
    vmem = pl.BlockSpec(memory_space=pltpu.VMEM)
    anywhere = pl.BlockSpec(memory_space=pl.ANY)
    bf, f32 = jnp.bfloat16, jnp.float32
    dma = pltpu.SemaphoreType.DMA
    return pl.pallas_call(
        functools.partial(expert_kernel, seqs, heads, chunks),
        out_shape=jax.ShapeDtypeStruct((rows, width), bf),
        in_specs=[pl.BlockSpec(memory_space=pltpu.SMEM)] + [vmem] * 4 + [anywhere] * 3,
        out_specs=vmem,
        scratch_shapes=[
            pltpu.VMEM((width, hidden), bf),
            pltpu.VMEM((width, hidden), bf),
            pltpu.VMEM((hidden, width), bf),
            pltpu.VMEM((heads, rows, width), bf),
            pltpu.VMEM((seqs, slots, width), bf),
            pltpu.VMEM((seqs, slots, width), bf),
            pltpu.VMEM((seqs, slots, width), bf),
            pltpu.VMEM((seqs * slots, hidden), f32),
            pltpu.VMEM((seqs * slots, hidden), f32),
            pltpu.VMEM((seqs * slots, hidden), bf),
            pltpu.VMEM((heads, rows, width), f32),
            pltpu.VMEM((heads, rows, width), bf),
            pltpu.VMEM((heads, rows, width), bf),
            dma((3, chunks)),
            dma((chunks, heads)),
            dma((chunks, heads)),
            dma((chunks, seqs)),
            dma((chunks, seqs)),
            dma((chunks, seqs)),
            dma((chunks, seqs)),
            dma((chunks, heads)),
            dma((chunks, heads)),
            dma((2, chunks)),
        ],
        compiler_params=pltpu.CompilerParams(
            collective_id=0, has_side_effects=True, vmem_limit_bytes=60 * 1024 * 1024
        ),
    )(scales, normed, residual, pick, mix, gate, up, down)


def attention_kernel(
    seqs,
    heads,
    halves,
    q_hbm,
    k_hbm,
    v_hbm,
    gain_ref,
    w_hbm,
    stream_hbm,
    model_ref,
    route_ref,
    res_ref,
    normed_ref,
    routes_ref,
    q_ref,
    k_ref,
    v_ref,
    stream_ref,
    state,
    mixed,
    normed_heads,
    wbuf,
    own,
    psend,
    precv,
    routes,
    sds,
    sdr,
    sfs,
    sfr,
    wds,
    wdr,
    wfs,
    wfr,
    zs,
    zr,
    gs,
    gr,
    lsem,
):
    s = lax.axis_index("seq")
    h = lax.axis_index("head")
    tokens = q_ref.shape[0]
    rows, width = stream_ref.shape
    bits = [2**i for i in range(1, seqs.bit_length() - 1)]
    orders = [bits, bits[::-1]]
    local = q_ref.shape[1] // HD
    block = w_hbm.shape[1]
    part = block // halves

    def flip(d):
        out, bit = s, 1
        while bit < seqs:
            if d & bit:
                out = out + bit * (1 - 2 * ((s // bit) % 2))
            bit *= 2
        return out

    partner = flip(1)

    def line(d):
        return lax.rem(h + d, heads)

    def remote(src, dst, ssem, rsem, seq, head):
        return pltpu.make_async_remote_copy(
            src_ref=src,
            dst_ref=dst,
            send_sem=ssem,
            recv_sem=rsem,
            device_id=(seq, head),
            device_id_type=MESH,
        )

    def state_direct(slot, peer):
        return remote(state.at[slot], state.at[slot], sds.at[peer], sdr.at[slot], peer, h)

    def state_pass(slot):
        return remote(state.at[slot], state.at[slot], sfs.at[slot], sfr.at[slot], partner, h)

    def w_at(slot, half):
        return wbuf.at[slot, :, pl.ds(half * part, part)]

    def w_first(half, bit):
        return remote(
            w_hbm.at[:, pl.ds(half * part, part)], w_at(s, half),
            wds.at[s, half, bits.index(bit)], wdr.at[s, half], flip(bit), h,
        )

    def w_relay(slot, half, bit):
        return remote(
            w_at(slot, half), w_at(slot, half),
            wds.at[slot, half, bits.index(bit)], wdr.at[slot, half], flip(bit), h,
        )

    def later_bits(d, half):
        order = orders[half]
        last = max(order.index(bit) for bit in bits if d & bit)
        return order[last + 1 :]

    def w_pass(slot, half):
        return remote(
            w_at(slot, half), w_at(slot, half), wfs.at[slot, half], wfr.at[slot, half], partner, h
        )

    def w_own_pass(half):
        return remote(
            w_hbm.at[:, pl.ds(half * part, part)], w_at(s, half),
            wfs.at[s, half], wfr.at[s, half], partner, h,
        )

    def w_own():
        return pltpu.make_async_copy(w_hbm, wbuf.at[s], lsem.at[0])

    def route_copy(slot, target):
        return remote(route_ref, routes.at[slot], gs.at[target], gr.at[slot], s, target)

    barrier = pltpu.get_barrier_semaphore()
    for d in range(1, seqs):
        pl.semaphore_signal(barrier, inc=1, device_id=(flip(d), h), device_id_type=MESH)
    for d in range(1, heads):
        pl.semaphore_signal(barrier, inc=1, device_id=(s, line(d)), device_id_type=MESH)
    loads = [
        pltpu.make_async_copy(source, target, lsem.at[1 + i])
        for i, (source, target) in enumerate(
            [(k_hbm, k_ref), (v_hbm, v_ref), (q_hbm, q_ref), (stream_hbm, stream_ref)]
        )
    ]
    for load in loads:
        load.start()
    w_own().start()
    routes[h] = route_ref[...]
    loads[0].wait()
    loads[1].wait()

    def lanes(i):
        return pl.ds(pl.multiple_of(i * HD, HD), HD)

    def block_state(i, carry):
        total = lax.dot_general(
            k_ref[:, lanes(i)], v_ref[:, lanes(i)], (((0,), (0,)), ((), ())),
            preferred_element_type=jnp.float32,
        )
        state[s, i] = total.astype(jnp.bfloat16)
        return carry

    lax.fori_loop(0, local, block_state, 0)
    pl.semaphore_wait(barrier, seqs + heads - 2)
    for d in range(2, seqs, 2):
        state_direct(s, flip(d)).start()
    state_pass(s).start()
    for d in range(1, heads):
        route_copy(h, line(d)).start()
    for i in range(len(bits)):
        for half in range(halves):
            w_first(half, orders[half][i]).start()
    for half in range(halves):
        w_own_pass(half).start()
    loads[2].wait()

    row = lax.broadcasted_iota(jnp.int32, (tokens, tokens), 0)
    col = lax.broadcasted_iota(jnp.int32, (tokens, tokens), 1)
    causal = col <= row

    def local_part(i, carry):
        scores = lax.dot_general(
            q_ref[:, lanes(i)], k_ref[:, lanes(i)], (((1,), (1,)), ((), ())),
            preferred_element_type=jnp.float32,
        )
        scores = jnp.where(causal, scores, 0.0).astype(jnp.bfloat16)
        mixed[:, lanes(i)] = jnp.dot(
            scores, v_ref[:, lanes(i)], preferred_element_type=jnp.float32
        )
        return carry

    lax.fori_loop(0, local, local_part, 0)

    for d in range(2, seqs, 2):
        state_direct(flip(d), flip(d)).wait_recv()
        state_pass(flip(d)).start()
    for d in range(1, seqs, 2):
        state_pass(flip(d)).wait_recv()

    def earlier_part(i, carry):
        prior = jnp.zeros((HD, HD), jnp.float32)
        for c in range(seqs):
            prior = prior + jnp.where(c < s, state[c, i].astype(jnp.float32), 0.0)
        total = mixed[:, lanes(i)] + jnp.dot(
            q_ref[:, lanes(i)], prior.astype(jnp.bfloat16), preferred_element_type=jnp.float32
        )
        mean_square = jnp.mean(total * total, axis=-1, keepdims=True)
        normed_heads[:, lanes(i)] = (
            total * lax.rsqrt(mean_square + 1e-06) * gain_ref[:, lanes(i)]
        ).astype(jnp.bfloat16)
        return carry

    lax.fori_loop(0, local, earlier_part, 0)

    def cols(slot, half):
        return pl.ds(pl.multiple_of(slot * block + half * part, part), part)

    def sum_copy(slot, half, d):
        return remote(
            psend.at[line(d), :, cols(slot, half)], precv.at[h, :, cols(slot, half)],
            zs.at[slot, half, d], zr.at[slot, half, h], s, line(d),
        )

    def sum_arrival(slot, half, source):
        return remote(
            psend.at[source, :, cols(slot, half)], precv.at[source, :, cols(slot, half)],
            zs.at[slot, half, 0], zr.at[slot, half, source], s, source,
        )

    def project(slot, half):
        total = jnp.dot(
            normed_heads[...],
            wbuf[slot, :, pl.ds(half * part, part)],
            preferred_element_type=jnp.float32,
        ).reshape(heads, rows, part)
        own[:, :, cols(slot, half)] = total
        psend[:, :, cols(slot, half)] = total.astype(jnp.bfloat16)
        for d in range(1, heads):
            sum_copy(slot, half, d).start()

    w_own().wait()
    evens = list(range(0, seqs, 2))
    schedule = []
    for low, high in zip(
        sorted(evens, key=lambda d: (d.bit_count(), d)),
        sorted(evens, key=lambda d: (d.bit_count(), -d)),
    ):
        schedule += [(low, 0), (high, 1)]
    for i in range(0, len(schedule), 2):
        pair = schedule[i : i + 2]
        for d, half in pair:
            if d:
                w_relay(flip(d), half, bits[0]).wait_recv()
                for bit in later_bits(d, half):
                    w_relay(flip(d), half, bit).start()
                w_pass(flip(d), half).start()
        for d, half in pair:
            project(flip(d), half)
        for d, half in pair:
            w_pass(flip(d + 1), half).wait_recv()
            project(flip(d + 1), half)

    def settle(i, carry):
        for half in range(halves):
            for d in range(1, heads):
                sum_arrival(i, half, line(d)).wait_recv()
        return carry

    lax.fori_loop(0, seqs, settle, 0)
    for d in range(1, heads):
        route_copy(line(d), line(d)).wait_recv()
    routes_ref[...] = routes[...]

    loads[3].wait()
    group = 16

    def normalise(i, carry):
        at = pl.ds(pl.multiple_of(i * group, group), group)
        total = own[h, at, :]
        for d in range(1, heads):
            total = total + precv[line(d), at, :].astype(jnp.float32)
        residual = (stream_ref[at, :].astype(jnp.float32) + total).astype(jnp.bfloat16)
        res_ref[at, :] = residual
        value = residual.astype(jnp.float32)
        mean_square = jnp.mean(value * value, axis=-1, keepdims=True)
        normed_ref[at, :] = (
            value * lax.rsqrt(mean_square + 1e-06) * model_ref[...]
        ).astype(jnp.bfloat16)
        return carry

    lax.fori_loop(0, rows // group, normalise, 0)

    for d in range(2, seqs, 2):
        state_direct(s, flip(d)).wait_send()
        for half in range(halves):
            for bit in later_bits(d, half):
                w_relay(flip(d), half, bit).wait_send()
    for half in range(halves):
        for bit in bits:
            w_first(half, bit).wait_send()
    for d in range(0, seqs, 2):
        state_pass(flip(d)).wait_send()
        for half in range(halves):
            if d:
                w_pass(flip(d), half).wait_send()
            else:
                w_own_pass(half).wait_send()
    for d in range(1, heads):
        route_copy(h, line(d)).wait_send()

    def drain(i, carry):
        for half in range(halves):
            for d in range(1, heads):
                sum_copy(i, half, d).wait_send()
        return carry

    lax.fori_loop(0, seqs, drain, 0)


def attention_call(seqs, heads, query, key, value, gain, weight, stream, model_gain, route):
    tokens, features = query.shape
    rows, width = stream.shape
    local = features // HD
    block = weight.shape[1]
    halves = 2
    vmem = pl.BlockSpec(memory_space=pltpu.VMEM)
    anywhere = pl.BlockSpec(memory_space=pl.ANY)
    bf, f32 = jnp.bfloat16, jnp.float32
    dma = pltpu.SemaphoreType.DMA
    return pl.pallas_call(
        functools.partial(attention_kernel, seqs, heads, halves),
        out_shape=(
            jax.ShapeDtypeStruct((rows, width), bf),
            jax.ShapeDtypeStruct((rows, width), bf),
            jax.ShapeDtypeStruct((heads,) + route.shape, f32),
        ),
        in_specs=[anywhere] * 3 + [vmem] + [anywhere] * 2 + [vmem] * 2,
        out_specs=(vmem,) * 3,
        scratch_shapes=[
            pltpu.VMEM((tokens, features), bf),
            pltpu.VMEM((tokens, features), bf),
            pltpu.VMEM((tokens, features), bf),
            pltpu.VMEM((rows, width), bf),
            pltpu.VMEM((seqs, local, HD, HD), bf),
            pltpu.VMEM((tokens, features), f32),
            pltpu.VMEM((tokens, features), bf),
            pltpu.VMEM((seqs, features, block), bf),
            pltpu.VMEM((heads, rows, width), f32),
            pltpu.VMEM((heads, rows, width), bf),
            pltpu.VMEM((heads, rows, width), bf),
            pltpu.VMEM((heads,) + route.shape, f32),
            dma((seqs,)),
            dma((seqs,)),
            dma((seqs,)),
            dma((seqs,)),
            dma((seqs, halves, seqs.bit_length())),
            dma((seqs, halves)),
            dma((seqs, halves)),
            dma((seqs, halves)),
            dma((seqs, halves, heads)),
            dma((seqs, halves, heads)),
            dma((heads,)),
            dma((heads,)),
            dma((5,)),
        ],
        compiler_params=pltpu.CompilerParams(
            collective_id=1, has_side_effects=True, vmem_limit_bytes=60 * 1024 * 1024
        ),
    )(
        query, key, value, gain.reshape(1, -1), weight, stream, model_gain.reshape(1, -1), route
    )


def routing(routed, seqs, heads):
    tok_rows = routed.shape[1]
    capacity = 3 * tok_rows * TOPK // (2 * seqs * heads)
    slots = -(-capacity * heads // 16) * 16
    routed = routed.reshape(-1, 2 * TOPK).T
    ids, gates = routed[:TOPK], routed[TOPK:]
    tokens = routed.shape[1]
    mine = (jnp.arange(seqs) * heads + lax.axis_index("head")).astype(jnp.float32)
    chosen = ids[None] == mine[:, None, None]
    hit = jnp.any(chosen, axis=1)
    weight = jnp.sum(jnp.where(chosen, gates[None], 0.0), axis=1)
    earlier = jnp.triu(jnp.ones((tokens, tokens), jnp.bfloat16), 1)
    rank = jnp.dot(hit.astype(jnp.bfloat16), earlier, preferred_element_type=jnp.float32)
    place = jnp.where(hit, rank, -1.0)
    slot = jnp.arange(slots, dtype=jnp.float32)
    taken = place[:, None, :] == slot[None, :, None]
    pick = taken.astype(jnp.bfloat16).reshape(seqs * slots, tokens)
    taken_t = place.T[:, :, None] == slot[None, None, :]
    mix = jnp.where(taken_t, weight.T[:, :, None], 0.0).astype(jnp.bfloat16)
    return pick, mix.reshape(tokens, seqs * slots)


def body(
    query,
    key,
    value,
    head_gain,
    out_weight,
    stream,
    model_gain,
    expert_ids,
    expert_gates,
    gate_weight,
    up_weight,
    down_weight,
    weight_scales,
):
    seqs, heads = lax.axis_size("seq"), lax.axis_size("head")
    route = jnp.concatenate([expert_ids.astype(jnp.float32), expert_gates], axis=1)
    residual, normed, routed = attention_call(
        seqs, heads, query, key, value, head_gain, out_weight, stream, model_gain, route
    )
    pick, mix = routing(routed, seqs, heads)
    return experts_call(
        seqs,
        heads,
        weight_scales,
        normed,
        residual,
        pick,
        mix,
        gate_weight,
        up_weight,
        down_weight,
    )


def solution(mesh):
    return jax.shard_map(
        body,
        mesh=mesh,
        in_specs=(
            P("seq", "head"),
            P("seq", "head"),
            P("seq", "head"),
            P("head"),
            P("head", "seq"),
            P(("seq", "head"), None),
            P(),
            P(("seq", "head"), None),
            P(("seq", "head"), None),
            P(("seq", "head"), None, None),
            P(("seq", "head"), None, None),
            P(("seq", "head"), None, None),
            P(("seq", "head"), None),
        ),
        out_specs=P(("seq", "head"), None),
        check_vma=False,
    )
```
